32 devices in a mesh: seg: 8 (over z, x), sub: 4 (over y, core).
Axes of the slice: x: 2, y: 2, z: 4, core: 2. Of those that a mesh axis runs over, the one named last changes fastest.
Arguments:
- leaf_mult: float32 [32768, 256], P(('seg', 'sub')), may hold values from -6 to 6
- m2m_ops: float32 [8, 256, 256], replicated, may hold values from -0.125 to 0.125
- m2l_ops: float32 [32, 256, 256], replicated, may hold values from -0.0625 to 0.0625
- owner_box: int32 [4096], P(('seg', 'sub')), may hold values from 0 to 4095, as said below
- src_list: int32 [4096, 32], P(('seg', 'sub')), may hold values from -1 to 4095, as said below
Outputs:
- parent_mult: float32 [4096, 256], P(('seg', 'sub'))
- owned_mult: float32 [4096, 256], P(('seg', 'sub'))
- local_exp: float32 [4096, 256], P(('seg', 'sub'))
The draws below stay inside these ranges and needn't reach their ends.
Inputs may be any that keep to these rules, and one draw needn't show every extreme that they name: `owner_box`: each aligned block of 512 rows, the g-th, holds every box id from g * 512 to (g + 1) * 512 - 1 once. `src_list`: A slot of a row in the g-th aligned block of 512 rows is -1 or names a box of the blocks g - 1, g or g + 1 of Morton order, each block being 512 consecutive ids.
All inputs are finite; a program needn't handle non-finite values.
Results may differ from the reference program's by a relative error of at most 0.000082.
Values sent between devices are 32-bit elements; how exact they have to be, the bound alone decides.
A program may use at most 64 MiB of HBM per device.

```python
import jax
import jax.numpy as jnp
from jax import lax

K = 256
SLOTS = 32
GROUP = 512
PARENTS = 4096
LEAVES = 32768
N_SEG = 8


def draw_owner_box(key, part):
    group_keys = jax.random.split(jax.random.fold_in(key, 11), N_SEG)
    orders = jax.vmap(lambda one_key: jax.random.permutation(one_key, GROUP))(group_keys)
    starts = (jnp.arange(N_SEG, dtype=jnp.int32) * GROUP)[:, None]
    return (orders.astype(jnp.int32) + starts).reshape(PARENTS)


def draw_src_list(key, part):
    pick_key, live_key = jax.random.split(jax.random.fold_in(key, 23))
    group_of = jnp.arange(PARENTS, dtype=jnp.int32) // GROUP
    low_end = jnp.maximum(group_of - 1, 0) * GROUP
    high_end = jnp.minimum(group_of + 2, N_SEG) * GROUP
    spans = (high_end - low_end)[:, None]
    chosen = jax.random.randint(pick_key, (PARENTS, SLOTS), 0, 1 << 30, dtype=jnp.int32) % spans + low_end[:, None]
    present = jax.random.randint(live_key, (PARENTS, SLOTS), 0, 4, dtype=jnp.int32) < 3
    result = jnp.where(present, chosen, -1)
    result = result.at[0, SLOTS - 1].set(-1)
    result = result.at[PARENTS - 1, 0].set(PARENTS - 1)
    return result.astype(jnp.int32)


def block_scale(key, extent, cuts, smallest, top_value):
    gain, own = 1.0, jax.random.fold_in(key, 6)
    for position, shards_of in cuts:
        steps = jnp.exp(jax.random.uniform(jax.random.fold_in(own, position), (shards_of,), jnp.float32, smallest / len(cuts), top_value / len(cuts)))
        gain = gain * jnp.repeat(steps, extent[position] // shards_of).reshape([-1 if axis == position else 1 for axis in range(len(extent))])
    return gain


def noise(key, extent, width, most, pieces=(), kind=jnp.bfloat16):
    drawn = width * jax.random.normal(key, extent, jnp.float32)
    if pieces:
        drawn = drawn * block_scale(key, extent, pieces, -0.22, 0.18)
    return jnp.clip(drawn, -most, most).astype(kind)


def setup_inputs(seed: int = 0) -> dict:
    arg_keys = jax.random.split(jax.random.key(seed), 6)
    return {
        "leaf_mult": noise(arg_keys[0], (LEAVES, K), 1.0, 6.0, ((0, 32),), jnp.float32),
        "m2m_ops": noise(arg_keys[1], (8, K, K), (8 * K) ** -0.5, 0.125, (), jnp.float32),
        "m2l_ops": noise(arg_keys[2], (SLOTS, K, K), (SLOTS * K) ** -0.5, 0.0625, (), jnp.float32),
        "owner_box": draw_owner_box(jax.random.fold_in(arg_keys[5], 71), 0),
        "src_list": draw_src_list(jax.random.fold_in(arg_keys[5], 71), 0),
    }


def reference(leaf_mult, m2m_ops, m2l_ops, owner_box, src_list):
    children = leaf_mult.reshape(PARENTS, 8, K)
    parent_mult = jnp.einsum('pck,ckl->pl', children, m2m_ops, precision=lax.Precision.HIGHEST)
    owned_mult = jnp.take(parent_mult, owner_box, axis=0)
    present = src_list >= 0
    clamped = jnp.where(present, src_list, 0)

    def translate(args):
        slot_rows, slot_live = args
        sources = jnp.take(parent_mult, slot_rows, axis=0)
        sources = jnp.where(slot_live[:, :, None], sources, jnp.float32(0.0))
        return jnp.einsum('rjk,jkl->rl', sources, m2l_ops, precision=lax.Precision.HIGHEST)

    blocks = lax.map(translate, (clamped.reshape(N_SEG, GROUP, SLOTS), present.reshape(N_SEG, GROUP, SLOTS)))
    local_exp = blocks.reshape(PARENTS, K)
    return parent_mult, owned_mult, local_exp
```

```python
import functools

import jax
import jax.numpy as jnp
from jax import lax
from jax.experimental import pallas as pl
from jax.experimental.pallas import tpu as pltpu
from jax.sharding import PartitionSpec as P

MESH = pl.DeviceIdType.MESH
LANES = 128
BATCH = 4


def split(value):
    high = value.astype(jnp.bfloat16)
    low = (value - high.astype(jnp.float32)).astype(jnp.bfloat16)
    return high, low


def kernel(
    n_seg, n_sub, parent, src_t, owner, ops_hbm, owned_out, local_out,
    pair, far, pair_parts, far_parts, ops, ops_high, ops_low, index, picked,
    ops_sem, own_sem, send_sem, recv_sem,
):
    seg, sub = lax.axis_index("seg"), lax.axis_index("sub")
    rows, width = parent.shape
    slots = src_t.shape[0]
    n_high = n_sub // 2
    side, core, high = seg % 2, sub % 2, sub // 2
    partner = seg + 1 - 2 * side
    other_side = 1 - side
    sibling = sub + 1 - 2 * core
    target = seg + 2 - 4 * side
    origin = seg - 2 + 4 * side
    has_target = (target >= 0) & (target < n_seg)
    has_origin = (origin >= 0) & (origin < n_seg)
    half = rows // 2
    group_rows = rows * n_sub

    ops_copy = pltpu.make_async_copy(ops_hbm, ops, ops_sem)
    ops_copy.start()

    barrier = pltpu.get_barrier_semaphore()

    def greet(to_seg, to_sub):
        pl.semaphore_signal(barrier, inc=1, device_id=(to_seg, to_sub), device_id_type=MESH)

    def peer(step):
        return lax.rem(high + step, n_high) * 2 + core

    greet(seg, sibling)
    greet(partner, sub)
    for step in range(1, n_high):
        greet(seg, peer(step))

    @pl.when(has_target)
    def _():
        greet(target, sub)

    @pl.when(has_origin)
    def _():
        greet(origin, sub)

    pl.semaphore_wait(barrier, 1 + n_high + has_target.astype(jnp.int32) + has_origin.astype(jnp.int32))

    names = {}

    def copy(name, src, dst, to_seg, to_sub):
        k = names.setdefault(name, len(names))
        return pltpu.make_async_remote_copy(
            src_ref=src, dst_ref=dst, send_sem=send_sem.at[k], recv_sem=recv_sem.at[k],
            device_id=(to_seg, to_sub), device_id_type=MESH,
        )

    def piece(part):
        return pl.ds(part * half, half)

    sent = []

    def go(c):
        c.start()
        sent.append(c)
        return c

    def to_x(part):
        return copy(("x", part), parent.at[piece(part)], pair.at[side, sub, piece(part)], partner, sub)

    def from_x(part):
        return copy(("x", part), parent.at[piece(part)], pair.at[other_side, sub, piece(part)], partner, sub)

    def to_y(step, part):
        return copy(("y", step, part), parent.at[piece(part)], pair.at[side, sub, piece(part)], seg, peer(step))

    def from_y(step, part):
        at = pair.at[side, peer(n_high - step), piece(part)]
        return copy(("y", step, part), parent.at[piece(part)], at, seg, peer(step))

    def xy(step):
        at = pair.at[other_side, sub, piece(0)]
        return copy(("xy", step), at, at, seg, peer(step))

    def from_xy(step):
        at = pair.at[other_side, peer(n_high - step), piece(0)]
        return copy(("xy", step), at, at, seg, peer(step))

    def yx(step):
        at = pair.at[side, peer(step), piece(1)]
        return copy(("yx", step), at, at, partner, sub)

    def from_yx(step):
        at = pair.at[other_side, peer(step), piece(1)]
        return copy(("yx", step), at, at, partner, sub)

    def z(step, part):
        return copy(
            ("z", step, part), pair.at[other_side, peer(step), piece(part)],
            far.at[peer(step), piece(part)], target, sub,
        )

    def to_sibling(step, which):
        at = far.at[peer(step)] if which == 2 else pair.at[(side, other_side)[which], peer(step)]
        src = parent if (step, which) == (0, 0) else at
        return copy(("s", step, which), src, at, seg, sibling)

    def from_sibling(step, which):
        s = lax.rem(high + step, n_high) * 2 + 1 - core
        at = far.at[s] if which == 2 else pair.at[(side, other_side)[which], s]
        return copy(("s", step, which), at, at, seg, sibling)

    go(to_x(0))
    for step in range(1, n_high):
        go(to_y(step, 1))
    go(to_x(1))
    for step in range(1, n_high):
        go(to_y(step, 0))
    go(to_sibling(0, 0))
    own = pltpu.make_async_copy(parent, pair.at[side, sub], own_sem)
    own.start()

    pad = jnp.full((LANES - slots - 8, rows), -1, jnp.int32)
    table = jnp.concatenate([src_t[...], jnp.broadcast_to(owner[...], (8, rows)), pad], axis=0)
    pair_start = (seg - side) * group_rows
    table = jnp.where(table < 0, -(1 << 28), table - pair_start)
    table = table.T
    for j in range(slots + 1):
        index[j] = jnp.broadcast_to(table[:, j : j + 1], (rows, LANES))

    from_x(0).wait_recv()
    for step in range(1, n_high):
        go(xy(step))

    @pl.when(has_target)
    def _():
        z(0, 0).start()

    for step in range(1, n_high):
        from_y(step, 1).wait_recv()
        go(yx(n_high - step))
    from_x(1).wait_recv()

    @pl.when(has_target)
    def _():
        z(0, 1).start()

    go(to_sibling(0, 1))
    for step in range(1, n_high):
        from_y(step, 0).wait_recv()
        go(to_sibling(n_high - step, 0))

    ops_copy.wait()

    def split_ops(start, stop):
        @pl.loop(start, stop)
        def _(j):
            ops_high[j], ops_low[j] = split(ops[j])

    split_ops(0, slots // 2)

    for step in range(1, n_high):
        from_xy(step).wait_recv()

        @pl.when(has_target)
        def _():
            z(n_high - step, 0).start()

    for step in range(1, n_high):
        from_yx(step).wait_recv()

        @pl.when(has_target)
        def _():
            z(step, 1).start()

        go(to_sibling(step, 1))

    split_ops(slots // 2, slots)

    own.wait()
    for step in range(n_high):
        from_sibling(step, 0).wait_recv()
    for step in range(n_high):
        from_sibling(step, 1).wait_recv()

    lane = lax.broadcasted_iota(jnp.int32, (1, LANES), 1)

    def one_hot(chosen, count, base):
        tiles = []
        for t in range(count // LANES):
            hit = chosen == lane + (base + t * LANES)
            tiles.append(jnp.where(hit, 1.0, 0.0).astype(jnp.bfloat16))
        return jnp.concatenate(tiles, axis=1)

    for s in range(2):
        for k in range(n_sub):
            at = pl.ds((s * n_sub + k) * rows, rows)
            pair_parts[at, :width], pair_parts[at, width:] = split(pair[s, k])

    chosen = index[slots]
    got = jnp.dot(one_hot(chosen, 2 * group_rows, 0), pair_parts[...], preferred_element_type=jnp.float32)
    owned_out[...] = got[:, :width] + got[:, width:]

    def near(start, stop):
        @pl.loop(start, stop)
        def _(b):
            chosen = index[pl.ds(b * BATCH, BATCH)].reshape(BATCH * rows, LANES)
            got = jnp.dot(
                one_hot(chosen, 2 * group_rows, 0), pair_parts[...], preferred_element_type=jnp.float32
            )
            picked[b] = got.astype(jnp.bfloat16)

    batches = slots // BATCH
    near(0, batches // 2)

    @pl.when(has_origin)
    def _():
        for step in range(n_high):
            for part in range(2):
                z(step, part).wait_recv()
            to_sibling(step, 2).start()

    near(batches // 2, batches)

    @pl.when(has_origin)
    def _():
        for step in range(n_high):
            from_sibling(step, 2).wait_recv()
        for k in range(n_sub):
            at = pl.ds(k * rows, rows)
            far_parts[at, :width], far_parts[at, width:] = split(far[k])

    far_base = -group_rows + side * (3 * group_rows)
    local_out[...] = jnp.zeros_like(local_out)

    def translate(with_far):
        @pl.loop(0, batches)
        def _(b):
            got = picked[b]
            if with_far:
                chosen = index[pl.ds(b * BATCH, BATCH)].reshape(BATCH * rows, LANES)
                more = jnp.dot(
                    one_hot(chosen, group_rows, far_base), far_parts[...], preferred_element_type=jnp.float32
                )
                got = got + more.astype(jnp.bfloat16)
            total = local_out[...]
            for i in range(BATCH):
                mine = got[i * rows : (i + 1) * rows]
                first, second = mine[:, :width], mine[:, width:]
                both = jnp.concatenate([first, second], axis=0)
                out = jnp.dot(both, ops_high[b * BATCH + i], preferred_element_type=jnp.float32)
                total = total + out[:rows] + out[rows:]
                total = total + jnp.dot(first, ops_low[b * BATCH + i], preferred_element_type=jnp.float32)
            local_out[...] = total

    @pl.when(has_origin)
    def _():
        translate(True)

    @pl.when(jnp.logical_not(has_origin))
    def _():
        translate(False)

    for c in sent:
        c.wait_send()

    @pl.when(has_target)
    def _():
        for step in range(n_high):
            for part in range(2):
                z(step, part).wait_send()

    @pl.when(has_origin)
    def _():
        for step in range(n_high):
            to_sibling(step, 2).wait_send()


def on_device(n_seg, n_sub, leaf_mult, m2m_ops, m2l_ops, owner_box, src_list):
    rows, width = leaf_mult.shape[0] // 8, leaf_mult.shape[1]
    slots = src_list.shape[1]
    children = leaf_mult.reshape(rows, 8, width)
    parent_mult = jnp.einsum("pck,ckl->pl", children, m2m_ops, precision=lax.Precision.HIGHEST)
    n_high = n_sub // 2
    messages = 2 + 4 * (n_high - 1) + 2 * n_high + 3 * n_high
    group_rows = rows * n_sub
    vmem = pl.BlockSpec(memory_space=pltpu.VMEM)
    half_type = jnp.bfloat16
    owned_mult, local_exp = pl.pallas_call(
        functools.partial(kernel, n_seg, n_sub),
        out_shape=[jax.ShapeDtypeStruct((rows, width), jnp.float32)] * 2,
        in_specs=[vmem, vmem, vmem, pl.BlockSpec(memory_space=pl.ANY)],
        out_specs=[vmem, vmem],
        scratch_shapes=[
            pltpu.VMEM((2, n_sub, rows, width), jnp.float32),
            pltpu.VMEM((n_sub, rows, width), jnp.float32),
            pltpu.VMEM((2 * group_rows, 2 * width), half_type),
            pltpu.VMEM((group_rows, 2 * width), half_type),
            pltpu.VMEM(m2l_ops.shape, jnp.float32),
            pltpu.VMEM(m2l_ops.shape, half_type),
            pltpu.VMEM(m2l_ops.shape, half_type),
            pltpu.VMEM((slots + 1, rows, LANES), jnp.int32),
            pltpu.VMEM((slots // BATCH, BATCH * rows, 2 * width), half_type),
            pltpu.SemaphoreType.DMA,
            pltpu.SemaphoreType.DMA,
            pltpu.SemaphoreType.DMA((messages,)),
            pltpu.SemaphoreType.DMA((messages,)),
        ],
        compiler_params=pltpu.CompilerParams(
            collective_id=0, has_side_effects=True, vmem_limit_bytes=60 << 20
        ),
    )(parent_mult, src_list.T, owner_box.reshape(1, rows), m2l_ops)
    return (parent_mult, owned_mult, local_exp)


def solution(mesh):
    n_seg, n_sub = mesh.shape["seg"], mesh.shape["sub"]
    in_specs = (P(("seg", "sub"), None), P(), P(), P(("seg", "sub")), P(("seg", "sub"), None))
    out_specs = (P(("seg", "sub"), None), P(("seg", "sub"), None), P(("seg", "sub"), None))
    return jax.shard_map(
        functools.partial(on_device, n_seg, n_sub),
        mesh=mesh, in_specs=in_specs, out_specs=out_specs, check_vma=False,
    )
```

```python
import functools

import jax
import jax.numpy as jnp
from jax import lax
from jax.experimental import pallas as pl
from jax.experimental.pallas import tpu as pltpu
from jax.sharding import PartitionSpec as P

MESH = pl.DeviceIdType.MESH
LANES = 128
BATCH = 4


def split(value):
    high = value.astype(jnp.bfloat16)
    low = (value - high.astype(jnp.float32)).astype(jnp.bfloat16)
    return high, low


def kernel(
    n_seg, n_sub, leaf_hbm, up_hbm, src_t, owner, ops_hbm, sums,
    leaf, up, parent,
    pair, far, pair_parts, far_parts, ops, ops_high, ops_low, index, picked,
    ops_sem, leaf_sem, up_sem, send_sem, recv_sem,
):
    seg, sub = lax.axis_index("seg"), lax.axis_index("sub")
    rows, width = parent.shape
    slots = src_t.shape[0]
    n_high = n_sub // 2
    side, core, high = seg % 2, sub % 2, sub // 2
    partner = seg + 1 - 2 * side
    other_side = 1 - side
    sibling = sub + 1 - 2 * core
    target = seg + 2 - 4 * side
    origin = seg - 2 + 4 * side
    has_target = (target >= 0) & (target < n_seg)
    has_origin = (origin >= 0) & (origin < n_seg)
    half = rows // 2
    group_rows = rows * n_sub

    n_up = up.shape[0]
    leaf_copies = [
        pltpu.make_async_copy(leaf_hbm.at[:, pl.ds(t * LANES, LANES)], leaf.at[t], leaf_sem.at[t])
        for t in range(width // LANES)
    ]
    for c in leaf_copies:
        c.start()
    up_copies = [pltpu.make_async_copy(up_hbm.at[c], up.at[c], up_sem.at[c]) for c in range(n_up)]
    for c in up_copies:
        c.start()
    ops_copy = pltpu.make_async_copy(ops_hbm, ops, ops_sem)
    ops_copy.start()

    barrier = pltpu.get_barrier_semaphore()

    def greet(to_seg, to_sub):
        pl.semaphore_signal(barrier, inc=1, device_id=(to_seg, to_sub), device_id_type=MESH)

    def peer(step):
        return lax.rem(high + step, n_high) * 2 + core

    greet(seg, sibling)
    greet(partner, sub)
    for step in range(1, n_high):
        greet(seg, peer(step))

    @pl.when(has_target)
    def _():
        greet(target, sub)

    @pl.when(has_origin)
    def _():
        greet(origin, sub)

    pad = jnp.full((LANES - slots - 8, rows), -1, jnp.int32)
    table = jnp.concatenate([src_t[...], jnp.broadcast_to(owner[...], (8, rows)), pad], axis=0)
    pair_start = (seg - side) * group_rows
    table = jnp.where(table < 0, -(1 << 28), table - pair_start)
    table = table.T
    for j in range(slots + 1):
        index[j] = jnp.broadcast_to(table[:, j : j + 1], (rows, LANES))

    def three_products(first, second, ops_first, ops_second):
        both = jnp.concatenate([first, second], axis=0)
        out = jnp.dot(both, ops_first, preferred_element_type=jnp.float32)
        return out[:rows] + out[rows:] + jnp.dot(first, ops_second, preferred_element_type=jnp.float32)

    for c in leaf_copies:
        c.wait()
    total = jnp.zeros((rows, width), jnp.float32)
    for c in range(n_up):
        up_copies[c].wait()
        child = jnp.concatenate(
            [leaf[t, pl.ds(c, rows, stride=n_up), :] for t in range(width // LANES)], axis=1
        )
        total = total + three_products(*split(child), *split(up[c]))
    parent[...] = total

    pl.semaphore_wait(barrier, 1 + n_high + has_target.astype(jnp.int32) + has_origin.astype(jnp.int32))

    names = {}

    def copy(name, src, dst, to_seg, to_sub):
        k = names.setdefault(name, len(names))
        return pltpu.make_async_remote_copy(
            src_ref=src, dst_ref=dst, send_sem=send_sem.at[k], recv_sem=recv_sem.at[k],
            device_id=(to_seg, to_sub), device_id_type=MESH,
        )

    def piece(part):
        return pl.ds(part * half, half)

    sent = []

    def go(c):
        c.start()
        sent.append(c)
        return c

    def to_x(part):
        return copy(("x", part), parent.at[piece(part)], pair.at[side, sub, piece(part)], partner, sub)

    def from_x(part):
        return copy(("x", part), parent.at[piece(part)], pair.at[other_side, sub, piece(part)], partner, sub)

    def to_y(step, part):
        return copy(("y", step, part), parent.at[piece(part)], pair.at[side, sub, piece(part)], seg, peer(step))

    def from_y(step, part):
        at = pair.at[side, peer(n_high - step), piece(part)]
        return copy(("y", step, part), parent.at[piece(part)], at, seg, peer(step))

    def xy(step):
        at = pair.at[other_side, sub, piece(0)]
        return copy(("xy", step), at, at, seg, peer(step))

    def from_xy(step):
        at = pair.at[other_side, peer(n_high - step), piece(0)]
        return copy(("xy", step), at, at, seg, peer(step))

    def yx(step):
        at = pair.at[side, peer(step), piece(1)]
        return copy(("yx", step), at, at, partner, sub)

    def from_yx(step):
        at = pair.at[other_side, peer(step), piece(1)]
        return copy(("yx", step), at, at, partner, sub)

    def z(step, part):
        return copy(
            ("z", step, part), pair.at[other_side, peer(step), piece(part)],
            far.at[peer(step), piece(part)], target, sub,
        )

    def to_sibling(step, which):
        at = far.at[peer(step)] if which == 2 else pair.at[(side, other_side)[which], peer(step)]
        src = parent if (step, which) == (0, 0) else at
        return copy(("s", step, which), src, at, seg, sibling)

    def from_sibling(step, which):
        s = lax.rem(high + step, n_high) * 2 + 1 - core
        at = far.at[s] if which == 2 else pair.at[(side, other_side)[which], s]
        return copy(("s", step, which), at, at, seg, sibling)

    go(to_x(0))
    for step in range(1, n_high):
        go(to_y(step, 1))
    go(to_x(1))
    for step in range(1, n_high):
        go(to_y(step, 0))
    go(to_sibling(0, 0))
    pair[side, sub] = parent[...]
    sums[0] = parent[...]

    from_x(0).wait_recv()
    for step in range(1, n_high):
        go(xy(step))

    @pl.when(has_target)
    def _():
        z(0, 0).start()

    for step in range(1, n_high):
        from_y(step, 1).wait_recv()
        go(yx(n_high - step))
    from_x(1).wait_recv()

    @pl.when(has_target)
    def _():
        z(0, 1).start()

    go(to_sibling(0, 1))
    for step in range(1, n_high):
        from_y(step, 0).wait_recv()
        go(to_sibling(n_high - step, 0))

    ops_copy.wait()

    def split_ops(start, stop):
        @pl.loop(start, stop)
        def _(j):
            ops_high[j], ops_low[j] = split(ops[j])

    split_ops(0, slots // 2)

    for step in range(1, n_high):
        from_xy(step).wait_recv()

        @pl.when(has_target)
        def _():
            z(n_high - step, 0).start()

    for step in range(1, n_high):
        from_yx(step).wait_recv()

        @pl.when(has_target)
        def _():
            z(step, 1).start()

        go(to_sibling(step, 1))

    split_ops(slots // 2, slots)

    for step in range(n_high):
        from_sibling(step, 0).wait_recv()
    for step in range(n_high):
        from_sibling(step, 1).wait_recv()

    lane = lax.broadcasted_iota(jnp.int32, (1, LANES), 1)

    def one_hot(chosen, count, base):
        tiles = []
        for t in range(count // LANES):
            hit = chosen == lane + (base + t * LANES)
            tiles.append(jnp.where(hit, 1.0, 0.0).astype(jnp.bfloat16))
        return jnp.concatenate(tiles, axis=1)

    for s in range(2):
        for k in range(n_sub):
            at = pl.ds((s * n_sub + k) * rows, rows)
            pair_parts[at, :width], pair_parts[at, width:] = split(pair[s, k])

    chosen = index[slots]
    got = jnp.dot(one_hot(chosen, 2 * group_rows, 0), pair_parts[...], preferred_element_type=jnp.float32)
    sums[1] = got[:, :width]
    sums[2] = got[:, width:]

    def near(start, stop):
        @pl.loop(start, stop)
        def _(b):
            chosen = index[pl.ds(b * BATCH, BATCH)].reshape(BATCH * rows, LANES)
            got = jnp.dot(
                one_hot(chosen, 2 * group_rows, 0), pair_parts[...], preferred_element_type=jnp.float32
            )
            picked[b] = got.astype(jnp.bfloat16)

    batches = slots // BATCH
    near(0, batches // 2)

    @pl.when(has_origin)
    def _():
        for step in range(n_high):
            for part in range(2):
                z(step, part).wait_recv()
            to_sibling(step, 2).start()

    near(batches // 2, batches)

    @pl.when(has_origin)
    def _():
        for step in range(n_high):
            from_sibling(step, 2).wait_recv()
        for k in range(n_sub):
            at = pl.ds(k * rows, rows)
            far_parts[at, :width], far_parts[at, width:] = split(far[k])

    far_base = -group_rows + side * (3 * group_rows)
    sums[3] = jnp.zeros((rows, width), jnp.float32)
    sums[4] = jnp.zeros((rows, width), jnp.float32)

    def translate(with_far):
        @pl.loop(0, batches)
        def _(b):
            got = picked[b]
            if with_far:
                chosen = index[pl.ds(b * BATCH, BATCH)].reshape(BATCH * rows, LANES)
                more = jnp.dot(
                    one_hot(chosen, group_rows, far_base), far_parts[...], preferred_element_type=jnp.float32
                )
                got = got + more.astype(jnp.bfloat16)
            total, rest = sums[3], sums[4]
            for i in range(BATCH):
                mine = got[i * rows : (i + 1) * rows]
                first, second = mine[:, :width], mine[:, width:]
                both = jnp.concatenate([first, second], axis=0)
                out = jnp.dot(both, ops_high[b * BATCH + i], preferred_element_type=jnp.float32)
                total = total + out[:rows]
                rest = rest + out[rows:]
                rest = rest + jnp.dot(first, ops_low[b * BATCH + i], preferred_element_type=jnp.float32)
            sums[3], sums[4] = total, rest

    @pl.when(has_origin)
    def _():
        translate(True)

    @pl.when(jnp.logical_not(has_origin))
    def _():
        translate(False)

    for c in sent:
        c.wait_send()

    @pl.when(has_target)
    def _():
        for step in range(n_high):
            for part in range(2):
                z(step, part).wait_send()

    @pl.when(has_origin)
    def _():
        for step in range(n_high):
            to_sibling(step, 2).wait_send()


def on_device(n_seg, n_sub, leaf_mult, m2m_ops, m2l_ops, owner_box, src_list):
    rows, width = leaf_mult.shape[0] // 8, leaf_mult.shape[1]
    slots = src_list.shape[1]
    n_high = n_sub // 2
    messages = 2 + 4 * (n_high - 1) + 2 * n_high + 3 * n_high
    group_rows = rows * n_sub
    vmem = pl.BlockSpec(memory_space=pltpu.VMEM)
    hbm = pl.BlockSpec(memory_space=pl.ANY)
    half_type = jnp.bfloat16
    sums = pl.pallas_call(
        functools.partial(kernel, n_seg, n_sub),
        out_shape=jax.ShapeDtypeStruct((5, rows, width), jnp.float32),
        in_specs=[hbm, hbm, vmem, vmem, hbm],
        out_specs=vmem,
        scratch_shapes=[
            pltpu.VMEM((width // LANES, leaf_mult.shape[0], LANES), jnp.float32),
            pltpu.VMEM(m2m_ops.shape, jnp.float32),
            pltpu.VMEM((rows, width), jnp.float32),
            pltpu.VMEM((2, n_sub, rows, width), jnp.float32),
            pltpu.VMEM((n_sub, rows, width), jnp.float32),
            pltpu.VMEM((2 * group_rows, 2 * width), half_type),
            pltpu.VMEM((group_rows, 2 * width), half_type),
            pltpu.VMEM(m2l_ops.shape, jnp.float32),
            pltpu.VMEM(m2l_ops.shape, half_type),
            pltpu.VMEM(m2l_ops.shape, half_type),
            pltpu.VMEM((slots + 1, rows, LANES), jnp.int32),
            pltpu.VMEM((slots // BATCH, BATCH * rows, 2 * width), half_type),
            pltpu.SemaphoreType.DMA,
            pltpu.SemaphoreType.DMA((width // LANES,)),
            pltpu.SemaphoreType.DMA((m2m_ops.shape[0],)),
            pltpu.SemaphoreType.DMA((messages,)),
            pltpu.SemaphoreType.DMA((messages,)),
        ],
        compiler_params=pltpu.CompilerParams(
            collective_id=0, has_side_effects=True, vmem_limit_bytes=60 << 20
        ),
    )(leaf_mult, m2m_ops, src_list.T, owner_box.reshape(1, rows), m2l_ops)
    return (sums[0], sums[1] + sums[2], sums[3] + sums[4])


def solution(mesh):
    n_seg, n_sub = mesh.shape["seg"], mesh.shape["sub"]
    in_specs = (P(("seg", "sub"), None), P(), P(), P(("seg", "sub")), P(("seg", "sub"), None))
    out_specs = (P(("seg", "sub"), None), P(("seg", "sub"), None), P(("seg", "sub"), None))
    return jax.shard_map(
        functools.partial(on_device, n_seg, n_sub),
        mesh=mesh, in_specs=in_specs, out_specs=out_specs, check_vma=False,
    )
```

```python
import functools

import jax
import jax.numpy as jnp
from jax import lax
from jax.experimental import pallas as pl
from jax.experimental.pallas import tpu as pltpu
from jax.sharding import PartitionSpec as P

MESH = pl.DeviceIdType.MESH
LANES = 128
BATCH = 4


def split(value):
    high = value.astype(jnp.bfloat16)
    low = (value - high.astype(jnp.float32)).astype(jnp.bfloat16)
    return high, low


def kernel(
    n_seg, n_sub, leaf_hbm, up_hbm, src_t, owner, ops_hbm, sums,
    leaf, up, parent,
    pair, far, pair_parts, far_parts, ops, ops_high, ops_low, index, picked,
    ops_sem, leaf_sem, up_sem, send_sem, recv_sem,
):
    seg, sub = lax.axis_index("seg"), lax.axis_index("sub")
    rows, width = parent.shape
    slots = src_t.shape[0]
    n_high = n_sub // 2
    side, core, high = seg % 2, sub % 2, sub // 2
    partner = seg + 1 - 2 * side
    other_side = 1 - side
    sibling = sub + 1 - 2 * core
    target = seg + 2 - 4 * side
    origin = seg - 2 + 4 * side
    has_target = (target >= 0) & (target < n_seg)
    has_origin = (origin >= 0) & (origin < n_seg)
    half = rows // 2
    group_rows = rows * n_sub

    n_up = up.shape[0]
    leaf_copies = [
        pltpu.make_async_copy(leaf_hbm.at[:, pl.ds(t * LANES, LANES)], leaf.at[t], leaf_sem.at[t])
        for t in range(width // LANES)
    ]
    for c in leaf_copies:
        c.start()
    up_copies = [pltpu.make_async_copy(up_hbm.at[c], up.at[c], up_sem.at[c]) for c in range(n_up)]
    for c in up_copies:
        c.start()
    middle = slots // 2
    ops_copies = [
        pltpu.make_async_copy(ops_hbm.at[at], ops.at[at], ops_sem.at[k])
        for k, at in enumerate((pl.ds(0, middle), pl.ds(middle, slots - middle)))
    ]

    barrier = pltpu.get_barrier_semaphore()

    def greet(to_seg, to_sub):
        pl.semaphore_signal(barrier, inc=1, device_id=(to_seg, to_sub), device_id_type=MESH)

    def peer(step):
        return lax.rem(high + step, n_high) * 2 + core

    greet(seg, sibling)
    greet(partner, sub)
    for step in range(1, n_high):
        greet(seg, peer(step))

    @pl.when(has_target)
    def _():
        greet(target, sub)

    @pl.when(has_origin)
    def _():
        greet(origin, sub)

    pad = jnp.full((LANES - slots - 8, rows), -1, jnp.int32)
    table = jnp.concatenate([src_t[...], jnp.broadcast_to(owner[...], (8, rows)), pad], axis=0)
    pair_start = (seg - side) * group_rows
    table = jnp.where(table < 0, -(1 << 28), table - pair_start)
    table = table.T
    for j in range(slots + 1):
        index[j] = jnp.broadcast_to(table[:, j : j + 1], (rows, LANES))

    def three_products(first, second, ops_first, ops_second):
        both = jnp.concatenate([first, second], axis=0)
        out = jnp.dot(both, ops_first, preferred_element_type=jnp.float32)
        return out[:rows] + out[rows:] + jnp.dot(first, ops_second, preferred_element_type=jnp.float32)

    for c in leaf_copies:
        c.wait()
    total = jnp.zeros((rows, width), jnp.float32)
    for c in range(n_up):
        up_copies[c].wait()
        if c == n_up // 2:
            for one in ops_copies:
                one.start()
        child = jnp.concatenate(
            [leaf[t, pl.ds(c, rows, stride=n_up), :] for t in range(width // LANES)], axis=1
        )
        total = total + three_products(*split(child), *split(up[c]))
    parent[...] = total

    pl.semaphore_wait(barrier, 1 + n_high + has_target.astype(jnp.int32) + has_origin.astype(jnp.int32))

    names = {}

    def copy(name, src, dst, to_seg, to_sub):
        k = names.setdefault(name, len(names))
        return pltpu.make_async_remote_copy(
            src_ref=src, dst_ref=dst, send_sem=send_sem.at[k], recv_sem=recv_sem.at[k],
            device_id=(to_seg, to_sub), device_id_type=MESH,
        )

    def piece(part):
        return pl.ds(part * half, half)

    sent = []

    def go(c):
        c.start()
        sent.append(c)
        return c

    def to_x(part):
        return copy(("x", part), parent.at[piece(part)], pair.at[side, sub, piece(part)], partner, sub)

    def from_x(part):
        return copy(("x", part), parent.at[piece(part)], pair.at[other_side, sub, piece(part)], partner, sub)

    def to_y(step, part):
        return copy(("y", step, part), parent.at[piece(part)], pair.at[side, sub, piece(part)], seg, peer(step))

    def from_y(step, part):
        at = pair.at[side, peer(n_high - step), piece(part)]
        return copy(("y", step, part), parent.at[piece(part)], at, seg, peer(step))

    def xy(step):
        at = pair.at[other_side, sub, piece(0)]
        return copy(("xy", step), at, at, seg, peer(step))

    def from_xy(step):
        at = pair.at[other_side, peer(n_high - step), piece(0)]
        return copy(("xy", step), at, at, seg, peer(step))

    def yx(step):
        at = pair.at[side, peer(step), piece(1)]
        return copy(("yx", step), at, at, partner, sub)

    def from_yx(step):
        at = pair.at[other_side, peer(step), piece(1)]
        return copy(("yx", step), at, at, partner, sub)

    def z(step, part):
        return copy(
            ("z", step, part), pair.at[other_side, peer(step), piece(part)],
            far.at[peer(step), piece(part)], target, sub,
        )

    def to_sibling(step, which):
        at = far.at[peer(step)] if which == 2 else pair.at[(side, other_side)[which], peer(step)]
        src = parent if (step, which) == (0, 0) else at
        return copy(("s", step, which), src, at, seg, sibling)

    def from_sibling(step, which):
        s = lax.rem(high + step, n_high) * 2 + 1 - core
        at = far.at[s] if which == 2 else pair.at[(side, other_side)[which], s]
        return copy(("s", step, which), at, at, seg, sibling)

    go(to_x(0))
    for step in range(1, n_high):
        go(to_y(step, 1))
    go(to_x(1))
    for step in range(1, n_high):
        go(to_y(step, 0))
    go(to_sibling(0, 0))
    pair[side, sub] = parent[...]
    sums[0] = parent[...]

    def split_ops(start, stop):
        @pl.loop(start, stop)
        def _(j):
            ops_high[j], ops_low[j] = split(ops[j])

    ops_copies[0].wait()
    split_ops(0, middle)

    from_x(0).wait_recv()
    for step in range(1, n_high):
        go(xy(step))

    @pl.when(has_target)
    def _():
        z(0, 0).start()

    for step in range(1, n_high):
        from_y(step, 1).wait_recv()
        go(yx(n_high - step))
    from_x(1).wait_recv()

    @pl.when(has_target)
    def _():
        z(0, 1).start()

    go(to_sibling(0, 1))
    for step in range(1, n_high):
        from_y(step, 0).wait_recv()
        go(to_sibling(n_high - step, 0))

    for step in range(1, n_high):
        from_xy(step).wait_recv()

        @pl.when(has_target)
        def _():
            z(n_high - step, 0).start()

    for step in range(1, n_high):
        from_yx(step).wait_recv()

        @pl.when(has_target)
        def _():
            z(step, 1).start()

        go(to_sibling(step, 1))


    ops_copies[1].wait()
    split_ops(middle, slots)

    for step in range(n_high):
        from_sibling(step, 0).wait_recv()
    for step in range(n_high):
        from_sibling(step, 1).wait_recv()

    lane = lax.broadcasted_iota(jnp.int32, (1, LANES), 1)

    def one_hot(chosen, count, base):
        tiles = []
        for t in range(count // LANES):
            hit = chosen == lane + (base + t * LANES)
            tiles.append(jnp.where(hit, 1.0, 0.0).astype(jnp.bfloat16))
        return jnp.concatenate(tiles, axis=1)

    for s in range(2):
        for k in range(n_sub):
            at = pl.ds((s * n_sub + k) * rows, rows)
            pair_parts[at, :width], pair_parts[at, width:] = split(pair[s, k])

    chosen = index[slots]
    got = jnp.dot(one_hot(chosen, 2 * group_rows, 0), pair_parts[...], preferred_element_type=jnp.float32)
    sums[1] = got[:, :width]
    sums[2] = got[:, width:]

    def near(start, stop):
        @pl.loop(start, stop)
        def _(b):
            chosen = index[pl.ds(b * BATCH, BATCH)].reshape(BATCH * rows, LANES)
            got = jnp.dot(
                one_hot(chosen, 2 * group_rows, 0), pair_parts[...], preferred_element_type=jnp.float32
            )
            picked[b] = got.astype(jnp.bfloat16)

    batches = slots // BATCH
    near(0, batches // 2)

    @pl.when(has_origin)
    def _():
        for step in range(n_high):
            for part in range(2):
                z(step, part).wait_recv()
            to_sibling(step, 2).start()

    near(batches // 2, batches)

    @pl.when(has_origin)
    def _():
        for step in range(n_high):
            from_sibling(step, 2).wait_recv()
        for k in range(n_sub):
            at = pl.ds(k * rows, rows)
            far_parts[at, :width], far_parts[at, width:] = split(far[k])

    far_base = -group_rows + side * (3 * group_rows)
    sums[3] = jnp.zeros((rows, width), jnp.float32)
    sums[4] = jnp.zeros((rows, width), jnp.float32)

    def translate(with_far):
        @pl.loop(0, batches)
        def _(b):
            got = picked[b]
            if with_far:
                chosen = index[pl.ds(b * BATCH, BATCH)].reshape(BATCH * rows, LANES)
                more = jnp.dot(
                    one_hot(chosen, group_rows, far_base), far_parts[...], preferred_element_type=jnp.float32
                )
                got = got + more.astype(jnp.bfloat16)
            total, rest = sums[3], sums[4]
            for i in range(BATCH):
                mine = got[i * rows : (i + 1) * rows]
                first, second = mine[:, :width], mine[:, width:]
                both = jnp.concatenate([first, second], axis=0)
                out = jnp.dot(both, ops_high[b * BATCH + i], preferred_element_type=jnp.float32)
                total = total + out[:rows]
                rest = rest + out[rows:]
                rest = rest + jnp.dot(first, ops_low[b * BATCH + i], preferred_element_type=jnp.float32)
            sums[3], sums[4] = total, rest

    @pl.when(has_origin)
    def _():
        translate(True)

    @pl.when(jnp.logical_not(has_origin))
    def _():
        translate(False)

    for c in sent:
        c.wait_send()

    @pl.when(has_target)
    def _():
        for step in range(n_high):
            for part in range(2):
                z(step, part).wait_send()

    @pl.when(has_origin)
    def _():
        for step in range(n_high):
            to_sibling(step, 2).wait_send()


def on_device(n_seg, n_sub, leaf_mult, m2m_ops, m2l_ops, owner_box, src_list):
    rows, width = leaf_mult.shape[0] // 8, leaf_mult.shape[1]
    slots = src_list.shape[1]
    n_high = n_sub // 2
    messages = 2 + 4 * (n_high - 1) + 2 * n_high + 3 * n_high
    group_rows = rows * n_sub
    vmem = pl.BlockSpec(memory_space=pltpu.VMEM)
    hbm = pl.BlockSpec(memory_space=pl.ANY)
    half_type = jnp.bfloat16
    sums = pl.pallas_call(
        functools.partial(kernel, n_seg, n_sub),
        out_shape=jax.ShapeDtypeStruct((5, rows, width), jnp.float32),
        in_specs=[hbm, hbm, vmem, vmem, hbm],
        out_specs=vmem,
        scratch_shapes=[
            pltpu.VMEM((width // LANES, leaf_mult.shape[0], LANES), jnp.float32),
            pltpu.VMEM(m2m_ops.shape, jnp.float32),
            pltpu.VMEM((rows, width), jnp.float32),
            pltpu.VMEM((2, n_sub, rows, width), jnp.float32),
            pltpu.VMEM((n_sub, rows, width), jnp.float32),
            pltpu.VMEM((2 * group_rows, 2 * width), half_type),
            pltpu.VMEM((group_rows, 2 * width), half_type),
            pltpu.VMEM(m2l_ops.shape, jnp.float32),
            pltpu.VMEM(m2l_ops.shape, half_type),
            pltpu.VMEM(m2l_ops.shape, half_type),
            pltpu.VMEM((slots + 1, rows, LANES), jnp.int32),
            pltpu.VMEM((slots // BATCH, BATCH * rows, 2 * width), half_type),
            pltpu.SemaphoreType.DMA((2,)),
            pltpu.SemaphoreType.DMA((width // LANES,)),
            pltpu.SemaphoreType.DMA((m2m_ops.shape[0],)),
            pltpu.SemaphoreType.DMA((messages,)),
            pltpu.SemaphoreType.DMA((messages,)),
        ],
        compiler_params=pltpu.CompilerParams(
            collective_id=0, has_side_effects=True, vmem_limit_bytes=60 << 20
        ),
    )(leaf_mult, m2m_ops, src_list.T, owner_box.reshape(1, rows), m2l_ops)
    return (sums[0], sums[1] + sums[2], sums[3] + sums[4])


def solution(mesh):
    n_seg, n_sub = mesh.shape["seg"], mesh.shape["sub"]
    in_specs = (P(("seg", "sub"), None), P(), P(), P(("seg", "sub")), P(("seg", "sub"), None))
    out_specs = (P(("seg", "sub"), None), P(("seg", "sub"), None), P(("seg", "sub"), None))
    return jax.shard_map(
        functools.partial(on_device, n_seg, n_sub),
        mesh=mesh, in_specs=in_specs, out_specs=out_specs, check_vma=False,
    )
```

```python
import functools

import jax
import jax.numpy as jnp
from jax import lax
from jax.experimental import pallas as pl
from jax.experimental.pallas import tpu as pltpu
from jax.sharding import PartitionSpec as P

MESH = pl.DeviceIdType.MESH
LANES = 128
BATCH = 16
PARTS = 4


def split(value):
    high = value.astype(jnp.bfloat16)
    low = (value - high.astype(jnp.float32)).astype(jnp.bfloat16)
    return high, low


def kernel(
    n_seg, n_sub, leaf_hbm, up_hbm, src_t, owner, ops_hbm, sums,
    leaf, up, parent,
    pair, far, pair_parts, far_parts, ops, ops_high, ops_low, index, picked,
    ops_sem, leaf_sem, up_sem, send_sem, recv_sem,
):
    seg, sub = lax.axis_index("seg"), lax.axis_index("sub")
    rows, width = parent.shape
    slots = src_t.shape[0]
    n_high = n_sub // 2
    side, core, high = seg % 2, sub % 2, sub // 2
    partner = seg + 1 - 2 * side
    other_side = 1 - side
    sibling = sub + 1 - 2 * core
    target = seg + 2 - 4 * side
    origin = seg - 2 + 4 * side
    has_target = (target >= 0) & (target < n_seg)
    has_origin = (origin >= 0) & (origin < n_seg)
    half = rows // PARTS
    group_rows = rows * n_sub

    n_up = up.shape[0]
    leaf_copies = [
        pltpu.make_async_copy(leaf_hbm.at[:, pl.ds(t * LANES, LANES)], leaf.at[t], leaf_sem.at[t])
        for t in range(width // LANES)
    ]
    for c in leaf_copies:
        c.start()
    up_copies = [pltpu.make_async_copy(up_hbm.at[c], up.at[c], up_sem.at[c]) for c in range(n_up)]
    for c in up_copies:
        c.start()
    middle = slots // 2
    ops_copies = [
        pltpu.make_async_copy(ops_hbm.at[at], ops.at[at], ops_sem.at[k])
        for k, at in enumerate((pl.ds(0, middle), pl.ds(middle, slots - middle)))
    ]

    barrier = pltpu.get_barrier_semaphore()

    def greet(to_seg, to_sub):
        pl.semaphore_signal(barrier, inc=1, device_id=(to_seg, to_sub), device_id_type=MESH)

    def peer(step):
        return lax.rem(high + step, n_high) * 2 + core

    greet(seg, sibling)
    greet(partner, sub)
    for step in range(1, n_high):
        greet(seg, peer(step))

    @pl.when(has_target)
    def _():
        greet(target, sub)

    @pl.when(has_origin)
    def _():
        greet(origin, sub)

    pad = jnp.full((LANES - slots - 8, rows), -1, jnp.int32)
    table = jnp.concatenate([src_t[...], jnp.broadcast_to(owner[...], (8, rows)), pad], axis=0)
    pair_start = (seg - side) * group_rows
    table = jnp.where(table < 0, -(1 << 28), table - pair_start)
    table = table.T
    for j in range(slots + 1):
        index[j] = jnp.broadcast_to(table[:, j : j + 1], (rows, LANES))

    def three_products(first, second, ops_first, ops_second):
        both = jnp.concatenate([first, second], axis=0)
        out = jnp.dot(both, ops_first, preferred_element_type=jnp.float32)
        return out[:rows] + out[rows:] + jnp.dot(first, ops_second, preferred_element_type=jnp.float32)

    for c in leaf_copies:
        c.wait()
    total = jnp.zeros((rows, width), jnp.float32)
    for c in range(n_up):
        up_copies[c].wait()
        if c == n_up // 2:
            for one in ops_copies:
                one.start()
        child = jnp.concatenate(
            [leaf[t, pl.ds(c, rows, stride=n_up), :] for t in range(width // LANES)], axis=1
        )
        total = total + three_products(*split(child), *split(up[c]))
    parent[...] = total

    pl.semaphore_wait(barrier, 1 + n_high + has_target.astype(jnp.int32) + has_origin.astype(jnp.int32))

    names = {}

    def copy(name, src, dst, to_seg, to_sub):
        k = names.setdefault(name, len(names))
        return pltpu.make_async_remote_copy(
            src_ref=src, dst_ref=dst, send_sem=send_sem.at[k], recv_sem=recv_sem.at[k],
            device_id=(to_seg, to_sub), device_id_type=MESH,
        )

    def piece(part):
        return pl.ds(part * half, half)

    sent = []

    def go(c):
        c.start()
        sent.append(c)
        return c

    def to_x(part):
        return copy(("x", part), parent.at[piece(part)], pair.at[side, sub, piece(part)], partner, sub)

    def from_x(part):
        return copy(("x", part), parent.at[piece(part)], pair.at[other_side, sub, piece(part)], partner, sub)

    def to_y(step, part):
        return copy(("y", step, part), parent.at[piece(part)], pair.at[side, sub, piece(part)], seg, peer(step))

    def from_y(step, part):
        at = pair.at[side, peer(n_high - step), piece(part)]
        return copy(("y", step, part), parent.at[piece(part)], at, seg, peer(step))

    def xy(step, part):
        at = pair.at[other_side, sub, piece(part)]
        return copy(("xy", step, part), at, at, seg, peer(step))

    def from_xy(step, part):
        at = pair.at[other_side, peer(n_high - step), piece(part)]
        return copy(("xy", step, part), at, at, seg, peer(step))

    def yx(step, part):
        at = pair.at[side, peer(step), piece(part)]
        return copy(("yx", step, part), at, at, partner, sub)

    def from_yx(step, part):
        at = pair.at[other_side, peer(step), piece(part)]
        return copy(("yx", step, part), at, at, partner, sub)

    def z(step, part):
        return copy(
            ("z", step, part), pair.at[other_side, peer(step), piece(part)],
            far.at[peer(step), piece(part)], target, sub,
        )

    def to_sibling(step, which):
        at = far.at[peer(step)] if which == 2 else pair.at[(side, other_side)[which], peer(step)]
        src = parent if (step, which) == (0, 0) else at
        return copy(("s", step, which), src, at, seg, sibling)

    def from_sibling(step, which):
        s = lax.rem(high + step, n_high) * 2 + 1 - core
        at = far.at[s] if which == 2 else pair.at[(side, other_side)[which], s]
        return copy(("s", step, which), at, at, seg, sibling)

    for part in range(PARTS):
        go(to_x(part))
        for step in range(1, n_high):
            go(to_y(step, PARTS - 1 - part))
    go(to_sibling(0, 0))
    pair[side, sub] = parent[...]
    sums[0] = parent[...]

    def split_ops(start, stop):
        @pl.loop(start, stop)
        def _(j):
            ops_high[j], ops_low[j] = split(ops[j])

    ops_copies[0].wait()
    split_ops(0, middle)

    for part in range(PARTS):
        from_x(part).wait_recv()

        @pl.when(has_target)
        def _():
            z(0, part).start()

        for step in range(1, n_high):
            if part < PARTS // 2:
                go(xy(step, part))
        for step in range(1, n_high):
            from_y(step, PARTS - 1 - part).wait_recv()
            if part < PARTS // 2:
                go(yx(n_high - step, PARTS - 1 - part))

    go(to_sibling(0, 1))
    for step in range(1, n_high):
        go(to_sibling(n_high - step, 0))

    for part in range(PARTS // 2):
        for step in range(1, n_high):
            from_xy(step, part).wait_recv()

            @pl.when(has_target)
            def _():
                z(n_high - step, part).start()

            from_yx(step, PARTS - 1 - part).wait_recv()

            @pl.when(has_target)
            def _():
                z(step, PARTS - 1 - part).start()

    for step in range(1, n_high):
        go(to_sibling(step, 1))

    ops_copies[1].wait()
    split_ops(middle, slots)

    for step in range(n_high):
        from_sibling(step, 0).wait_recv()
    for step in range(n_high):
        from_sibling(step, 1).wait_recv()

    lane = lax.broadcasted_iota(jnp.int32, (1, LANES), 1)

    def one_hot(chosen, count, base):
        tiles = []
        for t in range(count // LANES):
            hit = chosen == lane + (base + t * LANES)
            tiles.append(jnp.where(hit, 1.0, 0.0).astype(jnp.bfloat16))
        return jnp.concatenate(tiles, axis=1)

    for s in range(2):
        for k in range(n_sub):
            at = pl.ds((s * n_sub + k) * rows, rows)
            pair_parts[at, :width], pair_parts[at, width:] = split(pair[s, k])

    chosen = index[slots]
    own_rows = pair_parts[pl.ds(pl.multiple_of(side * group_rows, LANES), group_rows), :]
    got = jnp.dot(one_hot(chosen, group_rows, side * group_rows), own_rows, preferred_element_type=jnp.float32)
    sums[1] = got[:, :width]
    sums[2] = got[:, width:]

    def near(start, stop):
        @pl.loop(start, stop)
        def _(b):
            chosen = index[pl.ds(b * BATCH, BATCH)].reshape(BATCH * rows, LANES)
            got = jnp.dot(
                one_hot(chosen, 2 * group_rows, 0), pair_parts[...], preferred_element_type=jnp.float32
            )
            picked[b] = got.astype(jnp.bfloat16)

    batches = slots // BATCH
    near(0, batches // 2)

    @pl.when(has_origin)
    def _():
        for step in range(n_high):
            for part in range(PARTS):
                z(step, part).wait_recv()
            to_sibling(step, 2).start()

    near(batches // 2, batches)

    @pl.when(has_origin)
    def _():
        for step in range(n_high):
            from_sibling(step, 2).wait_recv()
        for k in range(n_sub):
            at = pl.ds(k * rows, rows)
            far_parts[at, :width], far_parts[at, width:] = split(far[k])

    far_base = -group_rows + side * (3 * group_rows)
    sums[3] = jnp.zeros((rows, width), jnp.float32)
    sums[4] = jnp.zeros((rows, width), jnp.float32)

    def translate(with_far):
        @pl.loop(0, batches)
        def _(b):
            got = picked[b]
            if with_far:
                chosen = index[pl.ds(b * BATCH, BATCH)].reshape(BATCH * rows, LANES)
                more = jnp.dot(
                    one_hot(chosen, group_rows, far_base), far_parts[...], preferred_element_type=jnp.float32
                )
                got = got + more.astype(jnp.bfloat16)
            total, rest = sums[3], sums[4]
            for i in range(BATCH):
                mine = got[i * rows : (i + 1) * rows]
                first, second = mine[:, :width], mine[:, width:]
                both = jnp.concatenate([first, second], axis=0)
                out = jnp.dot(both, ops_high[b * BATCH + i], preferred_element_type=jnp.float32)
                total = total + out[:rows]
                rest = rest + out[rows:]
                rest = rest + jnp.dot(first, ops_low[b * BATCH + i], preferred_element_type=jnp.float32)
            sums[3], sums[4] = total, rest

    @pl.when(has_origin)
    def _():
        translate(True)

    @pl.when(jnp.logical_not(has_origin))
    def _():
        translate(False)

    for c in sent:
        c.wait_send()

    @pl.when(has_target)
    def _():
        for step in range(n_high):
            for part in range(PARTS):
                z(step, part).wait_send()

    @pl.when(has_origin)
    def _():
        for step in range(n_high):
            to_sibling(step, 2).wait_send()


def on_device(n_seg, n_sub, leaf_mult, m2m_ops, m2l_ops, owner_box, src_list):
    rows, width = leaf_mult.shape[0] // 8, leaf_mult.shape[1]
    slots = src_list.shape[1]
    n_high = n_sub // 2
    messages = PARTS * (3 * n_high - 1) + 3 * n_high
    group_rows = rows * n_sub
    vmem = pl.BlockSpec(memory_space=pltpu.VMEM)
    hbm = pl.BlockSpec(memory_space=pl.ANY)
    half_type = jnp.bfloat16
    sums = pl.pallas_call(
        functools.partial(kernel, n_seg, n_sub),
        out_shape=jax.ShapeDtypeStruct((5, rows, width), jnp.float32),
        in_specs=[hbm, hbm, vmem, vmem, hbm],
        out_specs=vmem,
        scratch_shapes=[
            pltpu.VMEM((width // LANES, leaf_mult.shape[0], LANES), jnp.float32),
            pltpu.VMEM(m2m_ops.shape, jnp.float32),
            pltpu.VMEM((rows, width), jnp.float32),
            pltpu.VMEM((2, n_sub, rows, width), jnp.float32),
            pltpu.VMEM((n_sub, rows, width), jnp.float32),
            pltpu.VMEM((2 * group_rows, 2 * width), half_type),
            pltpu.VMEM((group_rows, 2 * width), half_type),
            pltpu.VMEM(m2l_ops.shape, jnp.float32),
            pltpu.VMEM(m2l_ops.shape, half_type),
            pltpu.VMEM(m2l_ops.shape, half_type),
            pltpu.VMEM((slots + 1, rows, LANES), jnp.int32),
            pltpu.VMEM((slots // BATCH, BATCH * rows, 2 * width), half_type),
            pltpu.SemaphoreType.DMA((2,)),
            pltpu.SemaphoreType.DMA((width // LANES,)),
            pltpu.SemaphoreType.DMA((m2m_ops.shape[0],)),
            pltpu.SemaphoreType.DMA((messages,)),
            pltpu.SemaphoreType.DMA((messages,)),
        ],
        compiler_params=pltpu.CompilerParams(
            collective_id=0, has_side_effects=True, vmem_limit_bytes=60 << 20
        ),
    )(leaf_mult, m2m_ops, src_list.T, owner_box.reshape(1, rows), m2l_ops)
    return (sums[0], sums[1] + sums[2], sums[3] + sums[4])


def solution(mesh):
    n_seg, n_sub = mesh.shape["seg"], mesh.shape["sub"]
    in_specs = (P(("seg", "sub"), None), P(), P(), P(("seg", "sub")), P(("seg", "sub"), None))
    out_specs = (P(("seg", "sub"), None), P(("seg", "sub"), None), P(("seg", "sub"), None))
    return jax.shard_map(
        functools.partial(on_device, n_seg, n_sub),
        mesh=mesh, in_specs=in_specs, out_specs=out_specs, check_vma=False,
    )
```
